256 devices in a mesh: field: 2 (over z_hi), dom: 128 (over z_lo, y, x, core).
Axes of the slice: x: 4, y: 4, z: 8 (z_hi: 2, z_lo: 4; z = z_hi * 4 + z_lo), core: 2. Of those that a mesh axis runs over, the one named last changes fastest.
Arguments:
- state: float32 [9, 35, 32768], P(None, None, ('field', 'dom')), may hold values from -6 to 6
- star: float32 [3, 9, 9, 32768], P(None, None, None, ('field', 'dom')), may hold values from -2.4 to 2.4
- normals: float32 [4, 3, 32768], P(None, None, ('field', 'dom')), may hold values from -3.6 to 3.6
- speed: float32 [32768], P(('field', 'dom')), may hold values from 0.5 to 2
- stiffness: float32 [3, 35, 35], replicated, may hold values from -1 to 1
- face_proj: float32 [4, 35, 15], replicated, may hold values from -1 to 1
- face_lift: float32 [4, 15, 35], replicated, may hold values from -0.75 to 0.75
- rotations: float32 [3, 15, 15], replicated, may hold values from -1.5 to 1.5
- face_source: int32 [4, 32768], P(None, ('field', 'dom')), may hold values from 0 to 624, as said below
- face_orient: int32 [4, 32768], P(None, ('field', 'dom')), may hold values from 0 to 2
- halo_send: int32 [2, 8192], P(None, ('field', 'dom')), may hold values from 0 to 511
- partner_send: int32 [3, 4096], P(None, ('field', 'dom')), may hold values from 0 to 511
Outputs:
- state_out: float32 [9, 35, 32768], P(None, None, ('field', 'dom'))
The draws below stay inside these ranges and needn't reach their ends.
Inputs may be any that keep to these rules, and one draw needn't show every extreme that they name: `face_source`: positions 512 to 623 of a device's list are each read by exactly one face of that device, and every device has a face that reads the zero trace at 624.
All inputs are finite; a program needn't handle non-finite values.
Results may differ from the reference program's by a relative error of at most 0.0003.
Values sent between devices are 32-bit elements; how exact they have to be, the bound alone decides.
A program may use at most 64 MiB of HBM per device.

```python
import math
import jax
import jax.numpy as jnp
from jax import lax

QUANT = 9
BASIS = 35
FACE_BASIS = 15
ORDER = 5
ELEMS_DEV = 128
HALO = 32
CAP = 16
ELEMS = 32768
N_FIELD = 2
N_DOM = 128


def draw_face_source(key, part):
    count = N_FIELD * N_DOM
    faces = 4 * ELEMS_DEV
    remote = 2 * HALO + 3 * CAP

    def one_device(dev_key):
        key_order, key_local, key_edge = jax.random.split(dev_key, 3)
        order = jax.random.permutation(key_order, faces)
        local = jax.random.randint(key_local, (faces,), 0, faces)
        boundary = jax.random.randint(key_edge, (faces,), 0, 16) == 0
        filled = jnp.where(boundary, faces + remote, local)
        filled = filled.at[order[:remote]].set(faces + jnp.arange(remote))
        filled = filled.at[order[remote]].set(faces + remote)
        return filled.reshape(4, ELEMS_DEV)
    keys = jax.random.split(jax.random.fold_in(key, 7), count)
    blocks = jax.vmap(one_device)(keys)
    return jnp.moveaxis(blocks, 0, 1).reshape(4, count * ELEMS_DEV).astype(jnp.int32)


def set_ends(values, rng, least, high):
    spot = [jax.random.randint(jax.random.fold_in(rng, axis), (), 0, length) for axis, length in enumerate(values.shape)]
    widest = values.shape.index(max(values.shape))
    beside = spot[:widest] + [(spot[widest] + 1) % values.shape[widest]] + spot[widest + 1:]
    return values.at[tuple(spot)].set(least).at[tuple(beside)].set(high)


def block_scale(own_key, shape, cuts, least, high):
    def one(dim, blocks):
        heights = jax.random.uniform(jax.random.fold_in(jax.random.fold_in(own_key, 6), dim), (blocks,), jnp.float32, least / len(cuts), high / len(cuts))
        return jnp.repeat(jnp.exp(heights), shape[dim] // blocks).reshape((-1,) + (1,) * (len(shape) - dim - 1))

    gain = one(*cuts[0])
    for cut in cuts[1:]:
        gain = gain * one(*cut)
    return gain


def gaussian(key, extent, spread, reach, pieces=(), held_as=jnp.bfloat16):
    array = jax.random.normal(key, extent, jnp.float32) * spread
    if len(pieces) > 0:
        array = block_scale(key, extent, pieces, -0.22, 0.18) * array
    return jnp.clip(array, min=-reach, max=reach).astype(held_as)


def setup_inputs(seed: int = 0) -> dict:
    key_of = jax.random.split(jax.random.key(seed), 13)
    state = gaussian(key_of[0], (QUANT, BASIS, ELEMS), 1.0, 6.0, ((2, 256),), jnp.float32)
    star = gaussian(key_of[1], (3, QUANT, QUANT, ELEMS), 0.4, 2.4, ((3, 256),), jnp.float32)
    normals = gaussian(key_of[2], (4, 3, ELEMS), 0.6, 3.6, ((2, 256),), jnp.float32)
    speed = jnp.clip(jnp.exp(math.log(2.0) - 1.3862944 * jax.random.uniform(key_of[3], (ELEMS,), jnp.float32) ** block_scale(key_of[3], (ELEMS,), ((0, 256),), -0.2, 0.2)), 0.5, 2.0)
    stiffness = gaussian(key_of[4], (3, BASIS, BASIS), BASIS ** -0.5, 1.0, (), jnp.float32)
    face_proj = gaussian(key_of[5], (4, BASIS, FACE_BASIS), BASIS ** -0.5, 1.0, (), jnp.float32)
    face_lift = gaussian(key_of[6], (4, FACE_BASIS, BASIS), (4 * FACE_BASIS) ** -0.5, 0.75, (), jnp.float32)
    rotations = gaussian(key_of[7], (3, FACE_BASIS, FACE_BASIS), FACE_BASIS ** -0.5, 1.5, (), jnp.float32)
    face_source = draw_face_source(jax.random.fold_in(key_of[12], 71), 0)
    face_orient = set_ends(jax.random.randint(key_of[9], (4, ELEMS), 0, 3), jax.random.fold_in(key_of[9], 1), 0, 2).astype(jnp.int32)
    halo_send = set_ends(jax.random.randint(key_of[10], (2, HALO * N_FIELD * N_DOM), 0, 4 * ELEMS_DEV), jax.random.fold_in(key_of[10], 1), 0, (4 * ELEMS_DEV) - 1).astype(jnp.int32)
    partner_send = set_ends(jax.random.randint(key_of[11], (3, CAP * N_FIELD * N_DOM), 0, 4 * ELEMS_DEV), jax.random.fold_in(key_of[11], 1), 0, (4 * ELEMS_DEV) - 1).astype(jnp.int32)
    return {"state": state, "star": star, "normals": normals, "speed": speed, "stiffness": stiffness, "face_proj": face_proj, "face_lift": face_lift, "rotations": rotations, "face_source": face_source, "face_orient": face_orient, "halo_send": halo_send, "partner_send": partner_send}


step_length = 1.0
highest = lax.Precision.HIGHEST


def star_apply(matrices, values):
    summed = matrices[:, 0, None, :] * values[0][None]
    for p in range(1, values.shape[0]):
        summed = summed + matrices[:, p, None, :] * values[p][None]
    return summed


def star_stack(star, values):
    return jnp.stack([star_apply(star[d], values) for d in range(3)])


def predictor(source, star, stiffness, time_start, time_stop):
    deriv_level = source
    factor = 1.0
    integral = (time_stop - time_start) * deriv_level
    for k in range(1, ORDER):
        deriv_level = -jnp.einsum('dqle,dlb->qbe', star_stack(star, deriv_level), stiffness, precision=highest)
        factor = factor * (k + 1)
        integral = integral + ((time_stop ** (k + 1) - time_start ** (k + 1)) / factor) * deriv_level
    return integral


def project(integral, face_proj):
    traces = jnp.einsum('qle,jlk->qkje', integral, face_proj, precision=highest)
    return traces.reshape(traces.shape[0], traces.shape[1], -1)


def face_matrices(star, normals):
    summed = 0.5 * normals[None, None, :, 0, :] * star[0][:, :, None, :]
    for d in range(1, 3):
        summed = summed + 0.5 * normals[None, None, :, d, :] * star[d][:, :, None, :]
    return summed


def update(current, integral, buffer, star, flux_mats, speed, stiffness, face_lift, rotations, face_source, face_orient):
    elem_count = integral.shape[2]
    quant_count = buffer.shape[0]
    face_count = buffer.shape[1]
    own = buffer[:, :, :4 * elem_count].reshape(quant_count, face_count, 4, elem_count)
    gathered = buffer[:, :, face_source]
    neighbour = jnp.zeros_like(own)
    for h in range(3):
        turned = jnp.einsum('qkfe,km->qmfe', gathered, rotations[h], precision=highest)
        neighbour = neighbour + jnp.where((face_orient == h)[None, None], turned, 0.0)
    both_sides = own + neighbour
    fluxes = 0.5 * speed * (own - neighbour)
    for p in range(quant_count):
        fluxes = fluxes + flux_mats[:, p, None] * both_sides[p][None]
    lifted = jnp.einsum('qkfe,fkb->qbe', fluxes, face_lift, precision=highest)
    volume = jnp.einsum('dqle,dbl->qbe', star_stack(star, integral), stiffness, precision=highest)
    return current + volume - lifted


def split_devices(values, width):
    count = N_FIELD * N_DOM
    shaped = values.reshape(values.shape[:-1] + (count, width))
    return jnp.moveaxis(shaped, -2, 0)


def shift_lower(values):
    filler = jnp.zeros_like(values[:, :1])
    return jnp.concatenate([filler, values[:, :-1]], axis=1)


def shift_upper(values):
    filler = jnp.zeros_like(values[:, :1])
    return jnp.concatenate([values[:, 1:], filler], axis=1)


def reference(state, star, normals, speed, stiffness, face_proj, face_lift, rotations, face_source, face_orient, halo_send, partner_send):
    count = N_FIELD * N_DOM
    state_b = split_devices(state, ELEMS_DEV)
    star_b = split_devices(star, ELEMS_DEV)
    normals_b = split_devices(normals, ELEMS_DEV)
    speed_b = split_devices(speed, ELEMS_DEV)
    source_b = split_devices(face_source, ELEMS_DEV)
    orient_b = split_devices(face_orient, ELEMS_DEV)
    halo_b = split_devices(halo_send, HALO)
    partner_b = split_devices(partner_send, CAP)
    ocean_flag = jnp.arange(count, dtype=jnp.int32) < N_DOM
    half_step = 0.5 * step_length
    current = state_b
    for s in range(2):
        time_start = jnp.where(ocean_flag, s * half_step, 0.0).astype(jnp.float32)
        time_stop = time_start + half_step

        def first(inputs):
            initial, latest, star_block, block_start, block_stop, halo_block, partner_block, is_ocean = inputs
            source = jnp.where(is_ocean, initial, latest)
            integral = predictor(source, star_block, stiffness, block_start, block_stop)
            traces = project(integral, face_proj)
            outward = jnp.stack([traces[:, :, halo_block[0]], traces[:, :, halo_block[1]]])
            partner = jnp.stack([traces[:, :, partner_block[j]] for j in range(3)])
            return integral, outward, partner

        integrals, outwards, partners = lax.map(first, (state_b, current, star_b, time_start, time_stop, halo_b, partner_b, ocean_flag))
        grouped = outwards.reshape((N_FIELD, N_DOM) + outwards.shape[1:])
        from_left = shift_lower(grouped[:, :, 1]).reshape((count,) + grouped.shape[3:])
        from_right = shift_upper(grouped[:, :, 0]).reshape((count,) + grouped.shape[3:])
        other = partners.reshape((N_FIELD, N_DOM) + partners.shape[1:])[::-1]
        arrive_low = shift_lower(other[:, :, 2]).reshape((count,) + other.shape[3:])
        arrive_mid = other[:, :, 1].reshape((count,) + other.shape[3:])
        arrive_high = shift_upper(other[:, :, 0]).reshape((count,) + other.shape[3:])

        def second(inputs):
            latest, integral, left_in, right_in, low_in, mid_in, high_in, star_block, normal_block, speed_block, source_block, orient_block = inputs
            traces = project(integral, face_proj)
            zero_column = jnp.zeros(traces.shape[:2] + (1,), jnp.float32)
            buffer = jnp.concatenate([traces, left_in, right_in, low_in, mid_in, high_in, zero_column], axis=2)
            flux_mats = face_matrices(star_block, normal_block)
            return update(latest, integral, buffer, star_block, flux_mats, speed_block, stiffness, face_lift, rotations, source_block, orient_block)

        current = lax.map(second, (current, integrals, from_left, from_right, arrive_low, arrive_mid, arrive_high, star_b, normals_b, speed_b, source_b, orient_b))
    return jnp.moveaxis(current, 0, -2).reshape(state.shape)
```

```python
import functools

import jax
import jax.numpy as jnp
from jax import lax
from jax.experimental import pallas as pl
from jax.experimental.pallas import tpu as pltpu
from jax.sharding import PartitionSpec as P

Q, B, FB, NE = 9, 35, 15, 128
BP, LP = 40, 48
F32, BF16 = jnp.float32, jnp.bfloat16
HALF = 0.5
ROUTES = (
    (0, 32, 32, -1, False),
    (32, 32, 0, 1, False),
    (64, 16, 96, -1, True),
    (80, 16, 80, 0, True),
    (96, 16, 64, 1, True),
)


def coefs(t0, t1):
    out, fact = [], 1.0
    for k in range(5):
        fact *= k + 1
        out.append((t1 ** (k + 1) - t0 ** (k + 1)) / fact)
    return out


EARLY, LATE = coefs(0.0, HALF), coefs(HALF, 2 * HALF)


def split(x):
    hi = x.astype(BF16)
    return hi, (x - hi.astype(F32)).astype(BF16)


def mm(a, b):
    return jnp.dot(a, b, preferred_element_type=F32)


def kernel(
    state, star, normals, speed, stiff, proj, lift, rot, fsrc, forient, halo, part,
    out,
    d_buf, cur, integ, a_pred, a_vol, a_proj, a_lift, a_rot, pad, ipad,
    sel_send, sel_loc, sel_rem, fmat, trace, both_g, gath, flux, vol, send, recv,
    send_sem, recv_sem,
):
    g, i = lax.axis_index("field"), lax.axis_index("dom")
    count = lax.axis_size("dom")
    before, after = lax.rem(i + count - 1, count), lax.rem(i + 1, count)

    def device(step, other):
        return ((1 - g) if other else g, {-1: before, 0: i, 1: after}[step])

    barrier = pltpu.get_barrier_semaphore()
    for _, _, _, step, other in ROUTES:
        pl.semaphore_signal(barrier, inc=1, device_id=device(step, other),
                            device_id_type=pl.DeviceIdType.MESH)

    zrow = jnp.zeros((BP - B, NE), F32)
    for q in range(Q):
        s = jnp.concatenate([state[q], zrow], axis=0)
        d_buf[0, q] = s
        cur[q] = s
        integ[q, BP:LP] = jnp.zeros((LP - BP, NE), F32)

    pad[...] = jnp.zeros_like(pad)
    for d in range(3):
        pad[d, 0:B, 0:B] = stiff[d]
    pred = jnp.zeros((BP, 128), F32)
    volm = jnp.zeros((BP, 128), F32)
    for d in range(3):
        x = pad[d]
        xt = x.T[0:BP]
        x = x[0:BP]
        pred = pred - (pltpu.roll(xt, BP * d, 1) if d else xt)
        volm = volm + (pltpu.roll(x, BP * d, 1) if d else x)

    def put_wide(dst, m):
        hi, lo = split(m)
        z = jnp.zeros_like(lo)
        dst[...] = jnp.concatenate(
            [jnp.concatenate([hi, hi], axis=1), jnp.concatenate([lo, z], axis=1)], axis=0)

    def put_narrow(dst, m, width):
        hi, lo = split(m)
        hi2 = (hi.astype(F32) + pltpu.roll(hi.astype(F32), width, 1)).astype(BF16)
        dst[...] = jnp.concatenate([hi2, lo], axis=0)

    put_wide(a_pred, pred)
    put_wide(a_vol, volm)
    for f in range(4):
        pad[f] = jnp.zeros((128, 128), F32)
        pad[f, 0:B, 0:FB] = proj[f]
    rows = [pad[f].T[0:16] for f in range(4)]
    put_narrow(a_proj, jnp.concatenate(rows, axis=0), LP)
    m = jnp.zeros((BP, 128), F32)
    for f in range(4):
        pad[f] = jnp.zeros((128, 128), F32)
        pad[f, 0:FB, 0:B] = lift[f]
        x = pad[f].T[0:BP]
        m = m + (pltpu.roll(x, 16 * f, 1) if f else x)
    put_narrow(a_lift, m, 64)
    m = jnp.zeros((16, 128), F32)
    for h in range(3):
        pad[h] = jnp.zeros((128, 128), F32)
        pad[h, 0:FB, 0:FB] = rot[h]
        x = pad[h].T[0:16]
        m = m + (pltpu.roll(x, 16 * h, 1) if h else x)
    put_narrow(a_rot, m, 48)

    ipad[...] = jnp.full((8, 128), -1, jnp.int32)
    ipad[0:2, 0:32] = halo[...]
    ipad[2:5, 0:16] = part[...]
    rows8 = ipad[...]
    want = rows8[0:1]
    for r, off in ((1, 32), (2, 64), (3, 80), (4, 96)):
        want = jnp.maximum(want, pltpu.roll(rows8, off, 1)[r:r + 1])
    iota = lax.broadcasted_iota(jnp.int32, (512, 128), 0)
    sel_send[...] = jnp.where(iota == want, 1.0, 0.0).astype(BF16)
    riota = iota[0:128]
    not_first = jnp.where(i > 0, 1, 0)
    not_last = jnp.where(i < count - 1, 1, 0)
    low = (riota < 32) | ((riota >= 64) & (riota < 80))
    high = ((riota >= 32) & (riota < 64)) | ((riota >= 96) & (riota < 112))
    mid = (riota >= 80) & (riota < 96)
    live = jnp.where(low, not_first, jnp.where(high, not_last, jnp.where(mid, 1, 0)))
    rpos = jnp.where(live > 0, riota + 512, -1)
    for f in range(4):
        src = fsrc[f:f + 1, :]
        sel_loc[:, f * 128:(f + 1) * 128] = jnp.where(iota == src, 1.0, 0.0).astype(BF16)
        sel_rem[:, f * 128:(f + 1) * 128] = jnp.where(rpos == src, 1.0, 0.0).astype(BF16)

    for f in range(4):
        n = [0.5 * normals[f, d:d + 1, :] for d in range(3)]
        for q in range(Q):
            fmat[q, 0:Q, f * 128:(f + 1) * 128] = (
                n[0] * star[0, q] + n[1] * star[1, q] + n[2] * star[2, q])

    def star_apply(value, mat, emit):
        v = [value(p) for p in range(Q)]
        zpad = jnp.zeros((8, NE), F32)
        for q0 in range(0, Q, 2):
            qs = [q for q in (q0, q0 + 1) if q < Q]
            cols = []
            for q in qs:
                parts = []
                for d in range(3):
                    acc = star[d, q, 0:1, :] * v[0]
                    for p in range(1, Q):
                        acc = acc + star[d, q, p:p + 1, :] * v[p]
                    parts.append(acc)
                hi, lo = split(jnp.concatenate(parts + [zpad], axis=0))
                cols.append(jnp.concatenate([hi, lo], axis=0))
            x = cols[0] if len(cols) == 1 else jnp.concatenate(cols, axis=1)
            r = mm(mat, x)
            r = r[0:BP] + r[BP:2 * BP]
            for n, q in enumerate(qs):
                emit(q, r[:, n * NE:(n + 1) * NE])

    def copies(s):
        out_ = []
        for k, (r0, n, d0, step, other) in enumerate(ROUTES):
            out_.append(pltpu.make_async_remote_copy(
                src_ref=send.at[s, pl.ds(r0, n)],
                dst_ref=recv.at[s, pl.ds(d0, n)],
                send_sem=send_sem.at[s, k],
                recv_sem=recv_sem.at[s, k],
                device_id=device(step, other),
                device_id_type=pl.DeviceIdType.MESH,
            ))
        return out_

    for s in range(2):
        ocean = g == 0

        def coef(k):
            if s == 0:
                return EARLY[k]
            return jnp.where(ocean, LATE[k], EARLY[k]).astype(F32)

        if s == 1:
            for q in range(Q):
                st = jnp.concatenate([state[q], zrow], axis=0)
                d_buf[0, q] = jnp.where(ocean, st, cur[q])
        c0 = coef(0)
        for q in range(Q):
            integ[q, 0:BP] = c0 * d_buf[0, q]

        def level(k, _):
            here, there = lax.rem(k, 2), lax.rem(k + 1, 2)
            c = jnp.float32(0.0)
            for n in range(4):
                c = jnp.where(k == n, coef(n + 1), c)

            def emit(q, r):
                d_buf[there, q] = r
                integ[q, 0:BP] = integ[q, 0:BP] + c * r

            star_apply(lambda p: d_buf[here, p], a_pred[...], emit)
            return 0

        lax.fori_loop(0, 4, level, 0)

        for q0 in range(0, Q, 2):
            qs = [q for q in (q0, q0 + 1) if q < Q]
            cols = []
            for q in qs:
                hi, lo = split(integ[q])
                cols.append(jnp.concatenate([hi, lo, jnp.zeros((32, NE), BF16)], axis=0))
            x = cols[0] if len(cols) == 1 else jnp.concatenate(cols, axis=1)
            r = mm(a_proj[...], x)
            r = r[0:64] + r[64:128]
            for n, q in enumerate(qs):
                for f in range(4):
                    t = r[f * 16:(f + 1) * 16, n * NE:(n + 1) * NE]
                    trace[q, :, f * 128:(f + 1) * 128] = t
                    hi, lo = split(t)
                    both_g[q * 16:(q + 1) * 16, f * 128:(f + 1) * 128] = hi
                    both_g[144 + q * 16:144 + (q + 1) * 16, f * 128:(f + 1) * 128] = lo
        r = mm(both_g[...], sel_send[...])
        r = jnp.concatenate([r[0:144] + r[144:288], jnp.zeros((112, 128), F32)], axis=0)
        send[s] = r.T
        if s == 0:
            pl.semaphore_wait(barrier, len(ROUTES))
        ops = copies(s)
        for op in ops:
            op.start()

        gath[...] = mm(both_g[...], sel_loc[...])

        def emit_vol(q, r):
            cur[q] = cur[q] + r

        star_apply(lambda p: integ[p, 0:BP], a_vol[...], emit_vol)

        for op in ops:
            op.wait_recv()
        rt = jnp.concatenate([recv[s], jnp.zeros((16, 256), F32)], axis=0).T[0:144]
        hi, lo = split(rt)
        gath[...] = gath[...] + mm(jnp.concatenate([hi, lo], axis=0), sel_rem[...])

        for q in range(Q):
            ghi = gath[q * 16:(q + 1) * 16]
            glo = gath[144 + q * 16:144 + (q + 1) * 16]
            masked = []
            for x in (ghi, glo):
                for h in range(3):
                    hit = jnp.concatenate([forient[f:f + 1, :] for f in range(4)], axis=1) == h
                    masked.append(jnp.where(hit, x, 0.0).astype(BF16))
            masked.append(jnp.zeros((32, 512), BF16))
            r = mm(a_rot[...], jnp.concatenate(masked, axis=0))
            nb = r[0:16] + r[16:32]
            gath[q * 16:(q + 1) * 16] = trace[q] + nb
            gath[144 + q * 16:144 + (q + 1) * 16] = trace[q] - nb
        sp = 0.5 * speed[...].reshape(1, NE)
        for f in range(4):
            ln = slice(f * 128, (f + 1) * 128)
            sums = [gath[p * 16:(p + 1) * 16, ln] for p in range(Q)]
            for q in range(Q):
                acc = sp * gath[144 + q * 16:144 + (q + 1) * 16, ln]
                for p in range(Q):
                    acc = acc + fmat[q, p:p + 1, ln] * sums[p]
                hi, lo = split(acc)
                flux[f * 16:(f + 1) * 16, q * NE:(q + 1) * NE] = hi
                flux[64 + f * 16:64 + (f + 1) * 16, q * NE:(q + 1) * NE] = lo
        r = mm(a_lift[...], flux[...])
        r = r[0:BP] + r[BP:2 * BP]
        for q in range(Q):
            new = cur[q] - r[:, q * NE:(q + 1) * NE]
            if s == 0:
                cur[q] = new
            else:
                out[q] = new[0:B]
    for s in range(2):
        for op in copies(s):
            op.wait_send()


def local(*args):
    vmem = pl.BlockSpec(memory_space=pltpu.VMEM)
    scratch = [
        pltpu.VMEM((2, Q, BP, NE), F32),
        pltpu.VMEM((Q, BP, NE), F32),
        pltpu.VMEM((Q, LP, NE), F32),
        pltpu.VMEM((2 * BP, 256), BF16),
        pltpu.VMEM((2 * BP, 256), BF16),
        pltpu.VMEM((128, 128), BF16),
        pltpu.VMEM((2 * BP, 128), BF16),
        pltpu.VMEM((32, 128), BF16),
        pltpu.VMEM((4, 128, 128), F32),
        pltpu.VMEM((8, 128), jnp.int32),
        pltpu.VMEM((512, 128), BF16),
        pltpu.VMEM((512, 512), BF16),
        pltpu.VMEM((128, 512), BF16),
        pltpu.VMEM((Q, 16, 512), F32),
        pltpu.VMEM((Q, 16, 512), F32),
        pltpu.VMEM((288, 512), BF16),
        pltpu.VMEM((288, 512), F32),
        pltpu.VMEM((128, Q * NE), BF16),
        pltpu.VMEM((8, 128), F32),
        pltpu.VMEM((2, 128, 256), F32),
        pltpu.VMEM((2, 112, 256), F32),
        pltpu.SemaphoreType.DMA((2, 5)),
        pltpu.SemaphoreType.DMA((2, 5)),
    ]
    return pl.pallas_call(
        kernel,
        out_shape=jax.ShapeDtypeStruct((Q, B, NE), F32),
        in_specs=[vmem] * len(args),
        out_specs=vmem,
        scratch_shapes=scratch,
        compiler_params=pltpu.CompilerParams(
            collective_id=0, has_side_effects=True, vmem_limit_bytes=32 * 1024 * 1024),
    )(*args)


def solution(mesh):
    in_specs = (
        P(None, None, ("field", "dom")),
        P(None, None, None, ("field", "dom")),
        P(None, None, ("field", "dom")),
        P(("field", "dom")),
        P(),
        P(),
        P(),
        P(),
        P(None, ("field", "dom")),
        P(None, ("field", "dom")),
        P(None, ("field", "dom")),
        P(None, ("field", "dom")),
    )
    out_specs = P(None, None, ("field", "dom"))
    return jax.shard_map(local, mesh=mesh, in_specs=in_specs, out_specs=out_specs, check_vma=False)
```

```python
import functools

import jax
import jax.numpy as jnp
from jax import lax
from jax.experimental import pallas as pl
from jax.experimental.pallas import tpu as pltpu
from jax.sharding import PartitionSpec as P

Q, B, FB, NE = 9, 35, 15, 128
BP, LP = 40, 48
F32, BF16 = jnp.float32, jnp.bfloat16
HALF = 0.5
ROUTES = (
    (0, 32, 32, -1, False),
    (32, 32, 0, 1, False),
    (64, 16, 96, -1, True),
    (80, 16, 80, 0, True),
    (96, 16, 64, 1, True),
)


def coefs(t0, t1):
    out, fact = [], 1.0
    for k in range(5):
        fact *= k + 1
        out.append((t1 ** (k + 1) - t0 ** (k + 1)) / fact)
    return out


EARLY, LATE = coefs(0.0, HALF), coefs(HALF, 2 * HALF)


def split(x):
    hi = x.astype(BF16)
    return hi, (x - hi.astype(F32)).astype(BF16)


def mm(a, b):
    return jnp.dot(a, b, preferred_element_type=F32)


def kernel(
    state, star, normals, speed, stiff, proj, lift, rot, fsrc, forient, halo, part,
    out,
    d_buf, cur, integ, a_pred, a_vol, a_proj, a_lift, a_rot, pad, ipad,
    sel_send, sel_loc, sel_rem, fmat, trace, both_g, gath, flux, vol, send, recv,
    send_sem, recv_sem,
):
    g, i = lax.axis_index("field"), lax.axis_index("dom")
    count = lax.axis_size("dom")
    before, after = lax.rem(i + count - 1, count), lax.rem(i + 1, count)

    def device(step, other):
        return ((1 - g) if other else g, {-1: before, 0: i, 1: after}[step])

    barrier = pltpu.get_barrier_semaphore()
    for _, _, _, step, other in ROUTES:
        pl.semaphore_signal(barrier, inc=1, device_id=device(step, other),
                            device_id_type=pl.DeviceIdType.MESH)

    zrow = jnp.zeros((BP - B, NE), F32)
    for q in range(Q):
        s = jnp.concatenate([state[q], zrow], axis=0)
        d_buf[0, q] = s
        cur[q] = s
        integ[q, BP:LP] = jnp.zeros((LP - BP, NE), F32)

    pad[...] = jnp.zeros_like(pad)
    for d in range(3):
        pad[d, 0:B, 0:B] = stiff[d]
    pred = jnp.zeros((BP, 128), F32)
    volm = jnp.zeros((BP, 128), F32)
    for d in range(3):
        x = pad[d]
        xt = x.T[0:BP]
        x = x[0:BP]
        pred = pred - (pltpu.roll(xt, BP * d, 1) if d else xt)
        volm = volm + (pltpu.roll(x, BP * d, 1) if d else x)

    def put_wide(dst, m):
        hi, lo = split(m)
        z = jnp.zeros_like(lo)
        dst[...] = jnp.concatenate(
            [jnp.concatenate([hi, hi], axis=1), jnp.concatenate([lo, z], axis=1)], axis=0)

    def put_narrow(dst, m, width):
        hi, lo = split(m)
        hi2 = (hi.astype(F32) + pltpu.roll(hi.astype(F32), width, 1)).astype(BF16)
        dst[...] = jnp.concatenate([hi2, lo], axis=0)

    put_wide(a_pred, pred)
    put_wide(a_vol, volm)
    for f in range(4):
        pad[f, 0:16] = jnp.zeros((16, 128), F32)
        pad[f, 0:FB, 0:B] = proj[:, f, :]
    rows = [pad[f, 0:16] for f in range(4)]
    put_narrow(a_proj, jnp.concatenate(rows, axis=0), LP)
    m = jnp.zeros((BP, 128), F32)
    for f in range(4):
        pad[f] = jnp.zeros((128, 128), F32)
        pad[f, 0:FB, 0:B] = lift[:, f, :]
        x = pad[f].T[0:BP]
        m = m + (pltpu.roll(x, 16 * f, 1) if f else x)
    put_narrow(a_lift, m, 64)
    m = jnp.zeros((16, 128), F32)
    for h in range(3):
        pad[h] = jnp.zeros((128, 128), F32)
        pad[h, 0:FB, 0:FB] = rot[h]
        x = pad[h].T[0:16]
        m = m + (pltpu.roll(x, 16 * h, 1) if h else x)
    put_narrow(a_rot, m, 48)

    ipad[...] = jnp.full((8, 128), -1, jnp.int32)
    ipad[0:2, 0:32] = halo[...]
    ipad[2:5, 0:16] = part[...]
    rows8 = ipad[...]
    want = rows8[0:1]
    for r, off in ((1, 32), (2, 64), (3, 80), (4, 96)):
        want = jnp.maximum(want, pltpu.roll(rows8, off, 1)[r:r + 1])
    iota = lax.broadcasted_iota(jnp.int32, (512, 128), 0)
    sel_send[...] = jnp.where(iota == want, 1.0, 0.0).astype(BF16)
    riota = iota[0:128]
    not_first = jnp.where(i > 0, 1, 0)
    not_last = jnp.where(i < count - 1, 1, 0)
    low = (riota < 32) | ((riota >= 64) & (riota < 80))
    high = ((riota >= 32) & (riota < 64)) | ((riota >= 96) & (riota < 112))
    mid = (riota >= 80) & (riota < 96)
    live = jnp.where(low, not_first, jnp.where(high, not_last, jnp.where(mid, 1, 0)))
    rpos = jnp.where(live > 0, riota + 512, -1)
    for f in range(4):
        src = fsrc[f:f + 1, :]
        sel_loc[:, f * 128:(f + 1) * 128] = jnp.where(iota == src, 1.0, 0.0).astype(BF16)
        sel_rem[:, f * 128:(f + 1) * 128] = jnp.where(rpos == src, 1.0, 0.0).astype(BF16)

    for f in range(4):
        n = [0.5 * normals[d, f:f + 1, :] for d in range(3)]
        for q in range(Q):
            fmat[q, 0:Q, f * 128:(f + 1) * 128] = (
                n[0] * star[q, :, 0, :] + n[1] * star[q, :, 1, :] + n[2] * star[q, :, 2, :])

    def star_apply(value, mat, emit):
        v = [value(p) for p in range(Q)]
        zpad = jnp.zeros((8, NE), F32)
        for q0 in range(0, Q, 2):
            qs = [q for q in (q0, q0 + 1) if q < Q]
            cols = []
            for q in qs:
                parts = []
                for d in range(3):
                    acc = star[q, 0, d:d + 1, :] * v[0]
                    for p in range(1, Q):
                        acc = acc + star[q, p, d:d + 1, :] * v[p]
                    parts.append(acc)
                hi, lo = split(jnp.concatenate(parts + [zpad], axis=0))
                cols.append(jnp.concatenate([hi, lo], axis=0))
            x = cols[0] if len(cols) == 1 else jnp.concatenate(cols, axis=1)
            r = mm(mat, x)
            r = r[0:BP] + r[BP:2 * BP]
            for n, q in enumerate(qs):
                emit(q, r[:, n * NE:(n + 1) * NE])

    def copies(s):
        out_ = []
        for k, (r0, n, d0, step, other) in enumerate(ROUTES):
            out_.append(pltpu.make_async_remote_copy(
                src_ref=send.at[s, pl.ds(r0, n)],
                dst_ref=recv.at[s, pl.ds(d0, n)],
                send_sem=send_sem.at[s, k],
                recv_sem=recv_sem.at[s, k],
                device_id=device(step, other),
                device_id_type=pl.DeviceIdType.MESH,
            ))
        return out_

    for s in range(2):
        ocean = g == 0

        def coef(k):
            if s == 0:
                return EARLY[k]
            return jnp.where(ocean, LATE[k], EARLY[k]).astype(F32)

        if s == 1:
            for q in range(Q):
                st = jnp.concatenate([state[q], zrow], axis=0)
                d_buf[0, q] = jnp.where(ocean, st, cur[q])
        c0 = coef(0)
        for q in range(Q):
            integ[q, 0:BP] = c0 * d_buf[0, q]

        def level(k, _):
            here, there = lax.rem(k, 2), lax.rem(k + 1, 2)
            c = jnp.float32(0.0)
            for n in range(4):
                c = jnp.where(k == n, coef(n + 1), c)

            def emit(q, r):
                d_buf[there, q] = r
                integ[q, 0:BP] = integ[q, 0:BP] + c * r

            star_apply(lambda p: d_buf[here, p], a_pred[...], emit)
            return 0

        lax.fori_loop(0, 4, level, 0)

        for q0 in range(0, Q, 2):
            qs = [q for q in (q0, q0 + 1) if q < Q]
            cols = []
            for q in qs:
                hi, lo = split(integ[q])
                cols.append(jnp.concatenate([hi, lo, jnp.zeros((32, NE), BF16)], axis=0))
            x = cols[0] if len(cols) == 1 else jnp.concatenate(cols, axis=1)
            r = mm(a_proj[...], x)
            r = r[0:64] + r[64:128]
            for n, q in enumerate(qs):
                for f in range(4):
                    t = r[f * 16:(f + 1) * 16, n * NE:(n + 1) * NE]
                    trace[q, :, f * 128:(f + 1) * 128] = t
                    hi, lo = split(t)
                    both_g[q * 16:(q + 1) * 16, f * 128:(f + 1) * 128] = hi
                    both_g[144 + q * 16:144 + (q + 1) * 16, f * 128:(f + 1) * 128] = lo
        r = mm(both_g[...], sel_send[...])
        r = jnp.concatenate([r[0:144] + r[144:288], jnp.zeros((112, 128), F32)], axis=0)
        send[s] = r.T
        if s == 0:
            pl.semaphore_wait(barrier, len(ROUTES))
        ops = copies(s)
        for op in ops:
            op.start()

        gath[...] = mm(both_g[...], sel_loc[...])

        def emit_vol(q, r):
            cur[q] = cur[q] + r

        star_apply(lambda p: integ[p, 0:BP], a_vol[...], emit_vol)

        for op in ops:
            op.wait_recv()
        rt = jnp.concatenate([recv[s], jnp.zeros((16, 256), F32)], axis=0).T[0:144]
        hi, lo = split(rt)
        gath[...] = gath[...] + mm(jnp.concatenate([hi, lo], axis=0), sel_rem[...])

        for q in range(Q):
            ghi = gath[q * 16:(q + 1) * 16]
            glo = gath[144 + q * 16:144 + (q + 1) * 16]
            masked = []
            for x in (ghi, glo):
                for h in range(3):
                    hit = jnp.concatenate([forient[f:f + 1, :] for f in range(4)], axis=1) == h
                    masked.append(jnp.where(hit, x, 0.0).astype(BF16))
            masked.append(jnp.zeros((32, 512), BF16))
            r = mm(a_rot[...], jnp.concatenate(masked, axis=0))
            nb = r[0:16] + r[16:32]
            gath[q * 16:(q + 1) * 16] = trace[q] + nb
            gath[144 + q * 16:144 + (q + 1) * 16] = trace[q] - nb
        sp = 0.5 * speed[...].reshape(1, NE)
        for f in range(4):
            ln = slice(f * 128, (f + 1) * 128)
            sums = [gath[p * 16:(p + 1) * 16, ln] for p in range(Q)]
            for q in range(Q):
                acc = sp * gath[144 + q * 16:144 + (q + 1) * 16, ln]
                for p in range(Q):
                    acc = acc + fmat[q, p:p + 1, ln] * sums[p]
                hi, lo = split(acc)
                flux[f * 16:(f + 1) * 16, q * NE:(q + 1) * NE] = hi
                flux[64 + f * 16:64 + (f + 1) * 16, q * NE:(q + 1) * NE] = lo
        r = mm(a_lift[...], flux[...])
        r = r[0:BP] + r[BP:2 * BP]
        for q in range(Q):
            new = cur[q] - r[:, q * NE:(q + 1) * NE]
            if s == 0:
                cur[q] = new
            else:
                out[q] = new[0:B]
    for s in range(2):
        for op in copies(s):
            op.wait_send()


def local(state, star, normals, speed, stiff, proj, lift, rot, fsrc, forient, halo, part):
    args = (
        state, star.transpose(1, 2, 0, 3), normals.transpose(1, 0, 2), speed, stiff,
        proj.transpose(2, 0, 1), lift.transpose(1, 0, 2), rot, fsrc, forient, halo, part)
    vmem = pl.BlockSpec(memory_space=pltpu.VMEM)
    scratch = [
        pltpu.VMEM((2, Q, BP, NE), F32),
        pltpu.VMEM((Q, BP, NE), F32),
        pltpu.VMEM((Q, LP, NE), F32),
        pltpu.VMEM((2 * BP, 256), BF16),
        pltpu.VMEM((2 * BP, 256), BF16),
        pltpu.VMEM((128, 128), BF16),
        pltpu.VMEM((2 * BP, 128), BF16),
        pltpu.VMEM((32, 128), BF16),
        pltpu.VMEM((4, 128, 128), F32),
        pltpu.VMEM((8, 128), jnp.int32),
        pltpu.VMEM((512, 128), BF16),
        pltpu.VMEM((512, 512), BF16),
        pltpu.VMEM((128, 512), BF16),
        pltpu.VMEM((Q, 16, 512), F32),
        pltpu.VMEM((Q, 16, 512), F32),
        pltpu.VMEM((288, 512), BF16),
        pltpu.VMEM((288, 512), F32),
        pltpu.VMEM((128, Q * NE), BF16),
        pltpu.VMEM((8, 128), F32),
        pltpu.VMEM((2, 128, 256), F32),
        pltpu.VMEM((2, 112, 256), F32),
        pltpu.SemaphoreType.DMA((2, 5)),
        pltpu.SemaphoreType.DMA((2, 5)),
    ]
    return pl.pallas_call(
        kernel,
        out_shape=jax.ShapeDtypeStruct((Q, B, NE), F32),
        in_specs=[vmem] * len(args),
        out_specs=vmem,
        scratch_shapes=scratch,
        compiler_params=pltpu.CompilerParams(
            collective_id=0, has_side_effects=True, vmem_limit_bytes=32 * 1024 * 1024),
    )(*args)


def solution(mesh):
    in_specs = (
        P(None, None, ("field", "dom")),
        P(None, None, None, ("field", "dom")),
        P(None, None, ("field", "dom")),
        P(("field", "dom")),
        P(),
        P(),
        P(),
        P(),
        P(None, ("field", "dom")),
        P(None, ("field", "dom")),
        P(None, ("field", "dom")),
        P(None, ("field", "dom")),
    )
    out_specs = P(None, None, ("field", "dom"))
    return jax.shard_map(local, mesh=mesh, in_specs=in_specs, out_specs=out_specs, check_vma=False)
```
